512 devices in a mesh: section: 32 (over z_hi, x, y), expert: 16 (over z_lo, core).
Axes of the slice: x: 4, y: 4, z: 16 (z_hi: 2, z_lo: 8; z = z_hi * 8 + z_lo), core: 2. Of those that a mesh axis runs over, the one named last changes fastest.
Arguments:
- act_rows: bfloat16 [32, 2048, 2048], P('section', 'expert'), may hold values from -6 to 6
- cot_rows: bfloat16 [32, 2048, 2048], P('section', 'expert'), may hold values from -2.390625 to 2.390625
- expert_ids: int32 [32, 2048, 1], P('section', 'expert'), may hold values from 0 to 15; in each aligned block of 128 rows (0 to 127, 128 to 255, ..., all dimensions but the last counted through in order) at most 16 rows name the same one
- w_gate: bfloat16 [32, 16, 2048, 128], P('section', 'expert'), may hold values from -0.125 to 0.125
- w_up: bfloat16 [32, 16, 2048, 128], P('section', 'expert'), may hold values from -0.125 to 0.125
- w_down: bfloat16 [32, 16, 128, 2048], P('section', 'expert'), may hold values from -0.375 to 0.375
Outputs:
- act_grad: bfloat16 [32, 2048, 2048], P('section', 'expert')
- gate_grad: bfloat16 [32, 16, 2048, 128], P('section', 'expert')
- up_grad: bfloat16 [32, 16, 2048, 128], P('section', 'expert')
- down_grad: bfloat16 [32, 16, 128, 2048], P('section', 'expert')
The draws below stay inside these ranges and needn't reach their ends.
Inputs may be any that keep to these rules, and one draw needn't show every extreme that they name: `expert_ids`: within the 128 rows of one device no expert is named by more than 16 rows, a bound that some block reaches; every expert serves rows somewhere.
All inputs are finite; a program needn't handle non-finite values.
Results may differ from the reference program's by a relative error of at most 0.0049.
Values may be sent and summed in bfloat16 or wider, within the bound.
No kernel may reach another device: no remote copies, remote signals or barrier semaphores. Data moves between devices by JAX's collectives and lax.ppermute only.
A program may use at most 64 MiB of HBM per device.

```python
import math
import jax
import jax.numpy as jnp
import numpy as np
from jax import lax

D = 2048
FF = 256
ROWS_DEV = 128
FH = 128
CAP = 16
ROWS = 2048
HALF = 16
N_SECTION = 32
N_EXPERT = 16


def level_of(own_key, shape, split, smallest, top_value):
    factor_of = 1.0
    for dim, parts in split:
        draws = jax.random.uniform(jax.random.fold_in(jax.random.fold_in(own_key, 6), dim), (parts,), jnp.float32, smallest / len(split), top_value / len(split))
        factor_of = factor_of * jnp.repeat(jnp.exp(draws), shape[dim] // parts).reshape((-1,) + (1,) * (len(shape) - 1 - dim))
    return factor_of


def routed_block(own_key, own, number, rows, count, top, reach, lean):
    ranking = jax.random.permutation(own_key, count)
    heavy_load, usual = portions_of(count, rows * top, reach, lean, True), portions_of(count, rows * top, reach, lean, False)
    places = jnp.arange(count)

    def named(sizes, offset_by):
        used = int((sizes > 0).sum())
        fixed = max(1, used // 4)
        passed = fixed + (places - fixed + offset_by * (used - fixed)) % max(1, count - fixed)
        return jnp.zeros((count,), jnp.int32).at[ranking[jnp.where(places < fixed, places, passed)]].set(jnp.asarray(sizes, jnp.int32))

    sizes = jnp.where(number % 4 == 0, named(heavy_load, number // 4), named(usual, number - number // 4 - 1))
    mixed = jax.random.permutation(jax.random.fold_in(own, 3), count)
    giver, taker = mixed[0:count // 2 * 2:2], mixed[1:count // 2 * 2:2]
    room = jnp.minimum(sizes[giver] - 1, reach - sizes[taker]) // 2
    room = jnp.where((giver == ranking[0]) | (taker == ranking[0]) | (sizes[taker] == 0), 0, jnp.maximum(room, 0))
    passed = jax.random.randint(jax.random.fold_in(own, 4), (count // 2,), 0, 1 << 20) % (room + 1)
    sizes = sizes.at[giver].add(-passed).at[taker].add(passed)
    members = jnp.searchsorted(jnp.cumsum(sizes), jnp.arange(rows * top), side="right").astype(jnp.int32)
    table = members.reshape(top, rows).T
    table = table[jax.random.permutation(jax.random.fold_in(own, 1), rows)]
    offset_by = jax.random.randint(jax.random.fold_in(own, 2), (rows, 1), 0, top)
    return jnp.take_along_axis(table, (jnp.arange(top)[None, :] + offset_by) % top, axis=1)


def portions_of(count, total, reach, slope, full):
    weights = [(1 << 20) // math.isqrt(rank ** slope) + 1 for rank in range(1, count + 1)]
    largest = reach if full else min(reach, max(-(-total // count), total * weights[0] // sum(weights)))
    least = 1 if total - largest >= count - 1 else 0
    given, rest = [largest] + [least] * (count - 1), total - largest - least * (count - 1)
    while rest > 0:
        candidates = [i for i in range(1, count) if given[i] < largest] or [i for i in range(1, count) if given[i] < reach]
        whole, left = sum([weights[i] for i in candidates]), rest
        for i in candidates:
            more = min(reach - given[i], max(1, left * weights[i] // whole), rest)
            given[i] = given[i] + more
            rest = rest - more
    return np.array(given)


def noise(rng, dims, width, most, split=(), kind=jnp.bfloat16):
    factor_of = level_of(rng, dims, split, -0.22, 0.18) if split else 1.0
    result = jax.random.normal(rng, dims, jnp.float32) * width * factor_of
    return jnp.minimum(jnp.maximum(result, -most), most).astype(kind)


def setup_inputs(seed: int = 0) -> dict:
    key_of = jax.random.split(jax.random.key(seed), 7)
    act_rows = noise(key_of[0], (N_SECTION, ROWS, D), 1.0, 6.0, ((0, 32), (1, 16)))
    cot_rows = noise(key_of[1], (N_SECTION, ROWS, D), 0.4, 2.390625, ((0, 32), (1, 16)))
    expert_ids_keys = jax.random.split(jax.random.fold_in(key_of[2], 1), N_SECTION * ROWS // ROWS_DEV)
    expert_ids_turns = jax.random.permutation(jax.random.fold_in(key_of[2], 3), N_SECTION * ROWS // ROWS_DEV)
    expert_ids = jax.vmap(lambda own, number: routed_block(jax.random.fold_in(key_of[2], 2), own, number, ROWS_DEV, N_EXPERT, 1, CAP, 1))(expert_ids_keys, expert_ids_turns).reshape((N_SECTION, ROWS, 1))
    w_gate = noise(key_of[3], (N_SECTION, N_EXPERT, D, FH), D ** -0.5, 0.125, ((0, 32), (1, 16)))
    w_up = noise(key_of[4], (N_SECTION, N_EXPERT, D, FH), D ** -0.5, 0.125, ((0, 32), (1, 16)))
    w_down = noise(key_of[5], (N_SECTION, N_EXPERT, FH, D), FF ** -0.5, 0.375, ((0, 32), (1, 16)))
    return {"act_rows": act_rows, "cot_rows": cot_rows, "expert_ids": expert_ids, "w_gate": w_gate, "w_up": w_up, "w_down": w_down}


def expert_pass(act_buf, cot_buf, gate_full, up_full, down_full):
    gate_pre = jnp.dot(act_buf, gate_full, preferred_element_type=jnp.float32)
    up_pre = jnp.dot(act_buf, up_full, preferred_element_type=jnp.float32)
    sigma = jax.nn.sigmoid(gate_pre)
    activ = gate_pre * sigma
    hidden = (activ * up_pre).astype(jnp.bfloat16)
    hidden_grad = jnp.dot(cot_buf, down_full.T, preferred_element_type=jnp.float32)
    gate_delta = (hidden_grad * up_pre * sigma * (1.0 + gate_pre * (1.0 - sigma))).astype(jnp.bfloat16)
    up_delta = (hidden_grad * activ).astype(jnp.bfloat16)
    act_back = (jnp.dot(gate_delta, gate_full.T, preferred_element_type=jnp.float32)
                + jnp.dot(up_delta, up_full.T, preferred_element_type=jnp.float32)).astype(jnp.bfloat16)
    gate_sum = jnp.dot(act_buf.T, gate_delta, preferred_element_type=jnp.float32)
    up_sum = jnp.dot(act_buf.T, up_delta, preferred_element_type=jnp.float32)
    down_sum = jnp.dot(hidden.T, cot_buf, preferred_element_type=jnp.float32)
    return act_back, gate_sum, up_sum, down_sum


def section_pass(act_section, cot_section, route_ids, gate_full, up_full, down_full):
    blocks = route_ids.reshape(N_EXPERT, ROWS_DEV)
    onehot = (blocks[:, :, None] == jnp.arange(N_EXPERT, dtype=jnp.int32)[None, None, :]).astype(jnp.int32)
    ranks = jnp.cumsum(onehot, axis=1) - onehot
    slots = jnp.sum(ranks * onehot, axis=2)
    source = jnp.arange(N_EXPERT, dtype=jnp.int32)[:, None]
    places = (blocks * (N_EXPERT * CAP) + source * CAP + slots).reshape(-1).astype(jnp.int32)
    total = N_EXPERT * N_EXPERT * CAP
    act_buf = jnp.zeros((total, D), act_section.dtype).at[places].set(act_section).reshape(N_EXPERT, N_EXPERT * CAP, D)
    cot_buf = jnp.zeros((total, D), cot_section.dtype).at[places].set(cot_section).reshape(N_EXPERT, N_EXPERT * CAP, D)
    act_back, gate_sum, up_sum, down_sum = lax.map(
        lambda operands: expert_pass(*operands), (act_buf, cot_buf, gate_full, up_full, down_full))
    return act_back.reshape(total, D)[places], gate_sum, up_sum, down_sum


def reference(act_rows, cot_rows, expert_ids, w_gate, w_up, w_down):
    def layer_pass(layer_index):
        low_section = layer_index
        high_section = layer_index + HALF
        gate_full = jnp.concatenate([w_gate[low_section], w_gate[high_section]], axis=2)
        up_full = jnp.concatenate([w_up[low_section], w_up[high_section]], axis=2)
        down_full = jnp.concatenate([w_down[low_section], w_down[high_section]], axis=1)
        first_pass = section_pass(act_rows[low_section], cot_rows[low_section], expert_ids[low_section, :, 0],
                                gate_full, up_full, down_full)
        second_pass = section_pass(act_rows[high_section], cot_rows[high_section], expert_ids[high_section, :, 0],
                                 gate_full, up_full, down_full)
        gate_total = (first_pass[1] + second_pass[1]).astype(jnp.bfloat16)
        up_total = (first_pass[2] + second_pass[2]).astype(jnp.bfloat16)
        down_total = (first_pass[3] + second_pass[3]).astype(jnp.bfloat16)
        return (first_pass[0], second_pass[0],
                gate_total[:, :, :FH], gate_total[:, :, FH:],
                up_total[:, :, :FH], up_total[:, :, FH:],
                down_total[:, :FH, :], down_total[:, FH:, :])

    results = lax.map(layer_pass, jnp.arange(HALF, dtype=jnp.int32))
    act_grad = jnp.concatenate([results[0], results[1]], axis=0)
    gate_grad = jnp.concatenate([results[2], results[3]], axis=0)
    up_grad = jnp.concatenate([results[4], results[5]], axis=0)
    down_grad = jnp.concatenate([results[6], results[7]], axis=0)
    return act_grad, gate_grad, up_grad, down_grad
```

```python
import jax
import jax.numpy as jnp
from jax import lax
from jax.sharding import Mesh, PartitionSpec as P

PAIR = ("half", "expert")


def per_device(act_rows, cot_rows, expert_ids, w_gate, w_up, w_down):
    n_experts = lax.axis_size("expert")
    n_halves = lax.axis_size("half")
    peers = n_halves * n_experts
    row_count = act_rows.shape[1]
    width = act_rows.shape[2]
    capacity = 2 * row_count // n_experts
    gate_w, up_w, down_w = w_gate[0, 0], w_up[0, 0], w_down[0, 0]
    f32 = jnp.float32

    route_ids = expert_ids[0, :, 0]
    onehot = (route_ids[:, None] == jnp.arange(n_experts, dtype=jnp.int32)[None, :]).astype(
        jnp.int32
    )
    ranks = jnp.cumsum(onehot, axis=0) - onehot
    places = route_ids * capacity + jnp.sum(ranks * onehot, axis=1)

    slots = jnp.arange(peers * capacity, dtype=jnp.int32) % (n_experts * capacity)
    pick = (slots[:, None] == places[None, :]).astype(jnp.bfloat16)
    packed = jnp.concatenate([act_rows[0], cot_rows[0]], axis=1)
    send = jnp.dot(pick, packed, preferred_element_type=f32).astype(jnp.bfloat16)
    received = lax.all_to_all(
        send.reshape(peers, capacity, 2 * width), PAIR, split_axis=0, concat_axis=0, tiled=True
    ).reshape(-1, 2 * width)
    act_buf = received[:, :width]
    cot_buf = received[:, width:]

    gate_pre = jnp.dot(act_buf, gate_w, preferred_element_type=f32)
    up_pre = jnp.dot(act_buf, up_w, preferred_element_type=f32)
    last = (((1,), (1,)), ((), ()))
    hidden_grad = lax.dot_general(cot_buf, down_w, last, preferred_element_type=f32)
    sigma = jax.nn.sigmoid(gate_pre)
    activ = gate_pre * sigma
    hidden = (activ * up_pre).astype(jnp.bfloat16)
    gate_delta = (hidden_grad * up_pre * sigma * (1.0 + gate_pre * (1.0 - sigma))).astype(
        jnp.bfloat16
    )
    up_delta = (hidden_grad * activ).astype(jnp.bfloat16)
    back = (
        lax.dot_general(gate_delta, gate_w, last, preferred_element_type=f32)
        + lax.dot_general(up_delta, up_w, last, preferred_element_type=f32)
    ).astype(jnp.bfloat16)
    returned = lax.all_to_all(
        back.reshape(peers, capacity, width), PAIR, split_axis=0, concat_axis=0, tiled=True
    ).reshape(-1, width)
    act_grad = lax.dot_general(
        pick, returned, (((0,), (0,)), ((), ())), preferred_element_type=f32
    ).astype(jnp.bfloat16)

    rows = (((0,), (0,)), ((), ()))
    gate_grad = lax.dot_general(act_buf, gate_delta, rows, preferred_element_type=f32)
    up_grad = lax.dot_general(act_buf, up_delta, rows, preferred_element_type=f32)
    down_grad = lax.dot_general(hidden, cot_buf, rows, preferred_element_type=f32)
    return (
        act_grad[None],
        gate_grad.astype(jnp.bfloat16)[None, None],
        up_grad.astype(jnp.bfloat16)[None, None],
        down_grad.astype(jnp.bfloat16)[None, None],
    )


def solution(mesh):
    sections, experts = mesh.devices.shape
    split = Mesh(
        mesh.devices.reshape(2, sections // 2, experts), ("half", "layer", "expert")
    )
    rows = P(("half", "layer"), "expert", None)
    weights = P(("half", "layer"), "expert", None, None)
    return jax.shard_map(
        per_device,
        mesh=split,
        in_specs=(rows, rows, rows, weights, weights, weights),
        out_specs=(rows, weights, weights, weights),
        check_vma=False,
    )
```

```python
import jax
import jax.numpy as jnp
import numpy as np
from jax import lax
from jax.sharding import Mesh, PartitionSpec as P

RING = ("half", "z_lo")
NEAR = 4
F32 = jnp.float32
BF16 = jnp.bfloat16
LAST = (((1,), (1,)), ((), ()))
FIRST = (((0,), (0,)), ((), ()))


def shifted(value, axes, by):
    peers = lax.axis_size(axes)
    return lax.ppermute(value, axes, [(i, (i + by) % peers) for i in range(peers)])


def stacked(parts):
    return jnp.concatenate(parts, axis=0)


def per_device(act_rows, cot_rows, expert_ids, w_gate, w_up, w_down):
    ring = lax.axis_size(RING)
    chips = lax.axis_size("z_lo")
    cores = lax.axis_size("core")
    n_experts = chips * cores
    row_count = act_rows.shape[1]
    width = act_rows.shape[2]
    units = w_gate.shape[3]
    capacity = 2 * row_count // n_experts
    block = cores * capacity
    near = NEAR
    z = lax.axis_index(RING)
    core = lax.axis_index("core")
    act, cot = act_rows[0], cot_rows[0]

    route_ids = expert_ids[0, :, 0]
    onehot = (route_ids[:, None] == jnp.arange(n_experts, dtype=jnp.int32)[None, :]).astype(
        jnp.int32
    )
    ranks = jnp.cumsum(onehot, axis=0) - onehot
    places = route_ids * capacity + jnp.sum(ranks * onehot, axis=1)
    marks = jnp.broadcast_to(places.astype(BF16)[:, None], (row_count, 128))

    def slots_at(distances, start=z):
        lane = np.arange(block, dtype=np.int32)
        away = np.repeat(np.array(distances, np.int32) + ring, block)
        which = np.tile(lane // capacity, len(distances))
        rank = np.tile(lane % capacity, len(distances))
        chip = lax.rem(start + away, chips)
        expert = cores * chip + lax.rem(core + which, cores)
        return (expert * capacity + rank).astype(BF16)

    def picker(mark_rows, targets):
        return (mark_rows[:, :1] == targets[None, :]).astype(BF16)

    def chosen(pick, rows):
        return lax.dot_general(pick, rows, FIRST, preferred_element_type=F32).astype(BF16)

    def placed(pick, rows):
        return jnp.dot(pick, rows, preferred_element_type=F32)

    local_pick = picker(marks, slots_at((0,)))
    act_got = {(0, 0): chosen(local_pick, act)}
    cot_got = {(0, 0): chosen(local_pick, cot)}
    state = {way: (cot, jnp.concatenate([act, marks], axis=1)) for way in (1, -1)}
    far_targets = {}
    for way in (1, -1):
        targets = slots_at(tuple(way * i for i in range(chips - near + 1)))
        last = targets[(chips - near) * block :]
        last = last[:capacity] if way == 1 else last[capacity:]
        far_targets[way] = stacked([targets[: (chips - near) * block], last])
    for hop in range(1, near + 1):
        for way in (1, -1):
            cot_now = shifted(state[way][0], RING, way)
            state[way] = (cot_now, state[way][1])
        for way in (1, -1):
            act_now = shifted(state[way][1], RING, way)
            state[way] = (state[way][0], act_now)
        for way in (1, -1):
            cot_now, act_now = state[way]
            targets = far_targets[way] if hop == near else far_targets[way][:block]
            pick = picker(act_now[:, width:], targets)
            act_pick, cot_pick = chosen(pick, act_now[:, :width]), chosen(pick, cot_now)
            act_got[way, hop], cot_got[way, hop] = act_pick[:block], cot_pick[:block]
            if hop == near:
                state[way] = (act_pick, cot_pick)
    for more in range(chips - near, 0, -1):
        for way in (1, -1):
            act_pick, cot_pick = state[way]
            size = block if near + more < chips else capacity
            part = slice(more * block, more * block + size)
            sent = stacked([act_pick[part], cot_pick[part]])
            got = shifted(sent, RING, way * more)
            act_got[way, near + more], cot_got[way, near + more] = got[:size], got[size:]

    in_own = jnp.concatenate([w_gate[0, 0], w_up[0, 0]], axis=1)
    down_own = w_down[0, 0]
    in_other = shifted(in_own, "core", 1)
    down_other = shifted(down_own, "core", 1)
    in_w = jnp.concatenate([in_own, in_other], axis=1)
    down_w = stacked([down_own, down_other])
    in_w, down_w = lax.optimization_barrier((in_w, down_w))

    def gathered(keys):
        return stacked([act_got[key] for key in keys]), stacked([cot_got[key] for key in keys])

    def expert_work(act_buf, cot_buf):
        own = lax.broadcasted_iota(jnp.int32, (act_buf.shape[0], 1), 0) % block < capacity
        pre = jnp.dot(act_buf, in_w, preferred_element_type=F32)
        pre = jnp.where(own, pre[:, : 2 * units], pre[:, 2 * units :])
        hidden_grad = lax.dot_general(cot_buf, down_w, LAST, preferred_element_type=F32)
        hidden_grad = jnp.where(own, hidden_grad[:, :units], hidden_grad[:, units:])
        gate_pre, up_pre = pre[:, :units], pre[:, units:]
        sigma = jax.nn.sigmoid(gate_pre)
        activ = gate_pre * sigma
        hidden = (activ * up_pre).astype(BF16)
        gate_delta = (hidden_grad * up_pre * sigma * (1.0 + gate_pre * (1.0 - sigma))).astype(BF16)
        up_delta = (hidden_grad * activ).astype(BF16)

        def by_core(value):
            zero = jnp.zeros_like(value)
            halves = [jnp.where(own, value, zero), jnp.where(own, zero, value)]
            return jnp.concatenate(halves, axis=1)

        deltas = by_core(jnp.concatenate([gate_delta, up_delta], axis=1))
        return act_buf, deltas, by_core(hidden), cot_buf

    def groups_of(distance):
        ways = (0,) if distance == 0 else (1, -1)
        return [(way, distance) for way in ways]

    near_keys = [key for distance in range(near + 1) for key in groups_of(distance)]
    far_keys = [key for distance in range(chips, near, -1) for key in groups_of(distance)]
    gate = (1, chips)
    act_near, cot_near, act_got[gate] = lax.optimization_barrier(
        (*gathered(near_keys), act_got[gate])
    )

    def sent_back(keys, grad):
        back = lax.dot_general(grad[1], in_w, LAST, preferred_element_type=F32).astype(BF16)
        at = 0
        for way, distance in keys:
            part = back[at : at + block]
            at += block
            returned.append(shifted(part, RING, -way * distance) if distance else part)
            return_from.append(way * distance)
        return back

    returned, return_from = [], []
    near_grad = expert_work(act_near, cot_near)
    sent_back(near_keys, near_grad)
    far_grad = expert_work(*gathered(far_keys))
    far_back = sent_back([(1, chips)] + far_keys[2:], far_grad)
    own_slots = picker(marks, slots_at(tuple(return_from)))
    near_grad, far_grad, _ = lax.optimization_barrier((near_grad, far_grad, far_back))

    in_grad = down_grad = 0.0
    for act_buf, deltas, hidden, cot_buf in (near_grad, far_grad):
        in_part = lax.dot_general(act_buf, deltas, FIRST, preferred_element_type=F32)
        down_part = lax.dot_general(hidden, cot_buf, FIRST, preferred_element_type=F32)
        in_grad += in_part
        down_grad += down_part
    in_back = shifted(in_grad[:, 2 * units :], "core", 1)
    down_back = shifted(down_grad[units:], "core", 1)
    in_grad = (in_grad[:, : 2 * units] + in_back).astype(BF16)
    down_grad = (down_grad[:units] + down_back).astype(BF16)
    act_grad = placed(own_slots, stacked(returned)).astype(BF16)
    return (
        act_grad[None],
        in_grad[:, :units][None, None],
        in_grad[:, units:][None, None],
        down_grad[None, None],
    )


def solution(mesh):
    sections, experts = mesh.devices.shape
    split = Mesh(
        mesh.devices.reshape(2, sections // 2, experts // 2, 2),
        ("half", "layer", "z_lo", "core"),
    )
    rows = P(("half", "layer"), ("z_lo", "core"), None)
    weights = P(("half", "layer"), ("z_lo", "core"), None, None)
    return jax.shard_map(
        per_device,
        mesh=split,
        in_specs=(rows, rows, rows, weights, weights, weights),
        out_specs=(rows, weights, weights, weights),
        check_vma=False,
    )
```
